32 devices in a mesh: groups: 2 (over x), rows: 16 (over z, y, core).
Axes of the slice: x: 2, y: 2, z: 4, core: 2. Of those that a mesh axis runs over, the one named last changes fastest.
Arguments:
- tap_two: bfloat16 [6144, 1024], P(('groups', 'rows')), parts along dimension 0, may hold values from -6 to 6
- coarse_path: bfloat16 [6144, 256], P(('groups', 'rows')), parts along dimension 0, may hold values from -6 to 6
- proj_weight: bfloat16 [1024, 512], replicated, may hold values from -0.1875 to 0.1875
- proj_bias: float32 [512], replicated, may hold values from -3 to 3
- lift_weight: bfloat16 [512, 2048], replicated, may hold values from -0.25 to 0.25
- lift_bias: float32 [512], replicated, may hold values from -3 to 3
- merge_weight: bfloat16 [4608, 256], replicated, may hold values from -0.09375 to 0.09375
- out_weight: bfloat16 [256, 256], replicated, may hold values from -0.375 to 0.375
- out_bias: float32 [256], replicated, may hold values from -3 to 3
- first_inner_w: bfloat16 [2304, 256], replicated, may hold values from -0.125 to 0.125
- first_inner_b: float32 [256], replicated, may hold values from -3 to 3
- first_outer_w: bfloat16 [2304, 256], replicated, may hold values from -0.125 to 0.125
- first_outer_b: float32 [256], replicated, may hold values from -3 to 3
- second_inner_w: bfloat16 [2304, 256], replicated, may hold values from -0.125 to 0.125
- second_inner_b: float32 [256], replicated, may hold values from -3 to 3
- second_outer_w: bfloat16 [2304, 256], replicated, may hold values from -0.125 to 0.125
- second_outer_b: float32 [256], replicated, may hold values from -3 to 3
Outputs:
- united: bfloat16 [64, 384, 256], P(('groups', 'rows')), parts along dimension 0
The draws below stay inside these ranges and needn't reach their ends.
There are 2 independent parts, one for each index of `groups`. The reference program is written for one: setup_inputs(seed, part) draws one part's arguments, and reference() takes and returns one part's arrays. A program takes and returns all parts, laid end to end along the dimension named above; an argument that names none is the same for every part. Nothing has to cross between parts.
All inputs are finite; a program needn't handle non-finite values.
Results may differ from the reference program's by a relative error of at most 0.0075.
Values may be sent and summed in bfloat16 or wider, within the bound.
No kernel may reach another device: no remote copies, remote signals or barrier semaphores. Data moves between devices by JAX's collectives and lax.ppermute only.
A program may use at most 64 MiB of HBM per device.

```python
import jax
import jax.numpy as jnp

D = 1024
FEAT2 = 512
F = 256
GW = 192
GH = 16
TOKENS = 3072


def shard_levels(own_key, dims, pieces, least, top_value):
    gain, own = 1.0, jax.random.fold_in(own_key, 6)
    for dim, shards_of in pieces:
        steps = jnp.exp(jax.random.uniform(jax.random.fold_in(own, dim), (shards_of,), jnp.float32, least / len(pieces), top_value / len(pieces)))
        gain = gain * jnp.repeat(steps, dims[dim] // shards_of).reshape([-1 if axis == dim else 1 for axis in range(len(dims))])
    return gain


def centred(rng, extent, width, bound, cuts=(), dtype=jnp.bfloat16):
    entries = jax.random.normal(rng, extent, jnp.float32) * width
    if len(cuts) > 0:
        entries = shard_levels(rng, extent, cuts, -0.22, 0.18) * entries
    return jnp.clip(entries, min=-bound, max=bound).astype(dtype)


def setup_inputs(seed: int = 0, part: int = 0) -> dict:
    arg_keys = jax.random.split(jax.random.key(seed), 18)
    part_keys = jax.random.split(jax.random.fold_in(arg_keys[17], part), 18)
    return {
        "tap_two": centred(part_keys[0], (TOKENS, D), 1.0, 6.0, ((0, 16),)),
        "coarse_path": centred(part_keys[1], (TOKENS, F), 1.0, 6.0, ((0, 16),)),
        "proj_weight": centred(arg_keys[2], (D, FEAT2), D ** -0.5, 0.1875),
        "proj_bias": centred(arg_keys[3], (FEAT2,), 0.5, 3.0, (), jnp.float32),
        "lift_weight": centred(arg_keys[4], (FEAT2, 4 * FEAT2), FEAT2 ** -0.5, 0.25),
        "lift_bias": centred(arg_keys[5], (FEAT2,), 0.5, 3.0, (), jnp.float32),
        "merge_weight": centred(arg_keys[6], (9 * FEAT2, F), (9 * FEAT2) ** -0.5, 0.09375),
        "out_weight": centred(arg_keys[7], (F, F), F ** -0.5, 0.375),
        "out_bias": centred(arg_keys[8], (F,), 0.5, 3.0, (), jnp.float32),
        "first_inner_w": centred(arg_keys[9], (9 * F, F), (9 * F) ** -0.5, 0.125),
        "first_inner_b": centred(arg_keys[10], (F,), 0.5, 3.0, (), jnp.float32),
        "first_outer_w": centred(arg_keys[11], (9 * F, F), (9 * F) ** -0.5, 0.125),
        "first_outer_b": centred(arg_keys[12], (F,), 0.5, 3.0, (), jnp.float32),
        "second_inner_w": centred(arg_keys[13], (9 * F, F), (9 * F) ** -0.5, 0.125),
        "second_inner_b": centred(arg_keys[14], (F,), 0.5, 3.0, (), jnp.float32),
        "second_outer_w": centred(arg_keys[15], (9 * F, F), (9 * F) ** -0.5, 0.125),
        "second_outer_b": centred(arg_keys[16], (F,), 0.5, 3.0, (), jnp.float32),
    }


def conv_grid(grid, weight):
    height, across, channels = grid.shape
    padded = jnp.pad(grid, ((1, 1), (1, 1), (0, 0)))
    total = jnp.zeros((height * across, weight.shape[1]), jnp.float32)
    for offset_row in range(3):
        for offset_col in range(3):
            tap_index = offset_row * 3 + offset_col
            shifted = padded[offset_row:offset_row + height, offset_col:offset_col + across].reshape(height * across, channels)
            total = total + jnp.dot(shifted, weight[tap_index * channels:(tap_index + 1) * channels], preferred_element_type=jnp.float32)
    return total.reshape(height, across, weight.shape[1])


def enlarge(grown):
    upper = 0.25 * grown[:-2] + 0.75 * grown[1:-1]
    lower = 0.75 * grown[1:-1] + 0.25 * grown[2:]

    def sideways(band):
        return (0.25 * band[:, :-2] + 0.75 * band[:, 1:-1], 0.75 * band[:, 1:-1] + 0.25 * band[:, 2:])

    upper_left, upper_right = sideways(upper)
    lower_left, lower_right = sideways(lower)
    top_pair = jnp.stack([upper_left, upper_right], axis=2)
    bottom_pair = jnp.stack([lower_left, lower_right], axis=2)
    joined = jnp.stack([top_pair, bottom_pair], axis=1)
    height, across, channels = upper_left.shape
    return joined.reshape(2 * height, 2 * across, channels)


def residual_unit(value, inner_w, inner_b, outer_w, outer_b, extra):
    first_pass = conv_grid(jnp.maximum(value, 0), inner_w) + inner_b
    inner = jnp.maximum(first_pass, 0.0).astype(jnp.bfloat16)
    return conv_grid(inner, outer_w) + outer_b + value.astype(jnp.float32) + extra


def reference(tap_two, coarse_path, proj_weight, proj_bias, lift_weight, lift_bias, merge_weight, out_weight, out_bias, first_inner_w, first_inner_b, first_outer_w, first_outer_b, second_inner_w, second_inner_b, second_outer_w, second_outer_b):
    projected = (jnp.dot(tap_two, proj_weight, preferred_element_type=jnp.float32) + proj_bias).astype(jnp.bfloat16)
    lifted = jnp.dot(projected, lift_weight, preferred_element_type=jnp.float32).reshape(GH, GW, 2, 2, FEAT2) + lift_bias
    widened = lifted.transpose(0, 2, 1, 3, 4).reshape(2 * GH, 2 * GW, FEAT2).astype(jnp.bfloat16)
    reassembled = conv_grid(widened, merge_weight).astype(jnp.bfloat16)
    coarse_grid = coarse_path.reshape(GH, GW, F).astype(jnp.float32)
    padded = jnp.pad(coarse_grid, ((1, 1), (1, 1), (0, 0)), mode="edge")
    spread = enlarge(padded).astype(jnp.bfloat16)
    carried = (jnp.dot(spread.reshape(4 * GH * GW, F), out_weight, preferred_element_type=jnp.float32) + out_bias).reshape(2 * GH, 2 * GW, F)
    merged = residual_unit(reassembled, first_inner_w, first_inner_b, first_outer_w, first_outer_b, carried).astype(jnp.bfloat16)
    united = residual_unit(merged, second_inner_w, second_inner_b, second_outer_w, second_outer_b, 0.0).astype(jnp.bfloat16)
    return united
```

```python
import functools

import jax
import jax.numpy as jnp
from jax import lax
from jax.experimental import pallas as pl
from jax.experimental.pallas import tpu as pltpu
from jax.sharding import PartitionSpec as P

GW = 192
QUAD = 4
SEG = GW // QUAD
HALO = 3
SENT = 56
SLOT = 64

BF16, F32 = jnp.bfloat16, jnp.float32
VMEM = pl.BlockSpec(memory_space=pltpu.VMEM)
ANY = pl.BlockSpec(memory_space=pl.ANY)


def place():
    position = lax.axis_index("rows")
    return lax.rem(position, QUAD), lax.div(position, QUAD)


def project_kernel(tap, coarse, weight, bias, *rest):
    segments, (grid, sparse) = rest[:QUAD], rest[QUAD:]
    own, _ = place()
    edge = grid.shape[0] - GW
    grid[0:8] = jnp.zeros((8, grid.shape[1]), F32)
    grid[GW:] = jnp.zeros((edge, grid.shape[1]), F32)
    grid[HALO : HALO + GW] = jnp.dot(tap[...], weight[...], preferred_element_type=F32) + bias[...]
    wide = coarse[...].astype(F32)
    sparse[0:8] = jnp.zeros((8, sparse.shape[1]), F32)
    sparse[GW:] = jnp.zeros((edge, sparse.shape[1]), F32)
    sparse[HALO : HALO + GW] = wide
    sparse[HALO - 1 : HALO] = wide[:1]
    sparse[HALO + GW : HALO + GW + 1] = wide[GW - 1 :]
    split = grid.shape[1]
    for k in range(QUAD):
        start = pl.multiple_of(lax.bitwise_xor(own, k) * SEG, 16)
        segments[k][:, :split] = grid[pl.ds(start, SENT), :].astype(BF16)
        segments[k][:, split:] = sparse[pl.ds(start, SENT), :].astype(BF16)


def pack_kernel(split, *refs):
    segments, (block, first, second) = refs[:QUAD], refs[QUAD:]
    own, number = place()
    for row in range(QUAD):
        for k in range(QUAD):

            @pl.when(own == row ^ k)
            def _():
                block[row * SENT : (row + 1) * SENT] = segments[k][...]

    coarse = block.shape[1] - split
    even = lax.rem(number, 2) == 0

    def fill(payload, row, coarse_row):
        payload[: HALO * SENT] = block[row * SENT : (row + HALO) * SENT, :split]
        for half in range(2):
            payload[HALO * SENT :, half * coarse : (half + 1) * coarse] = block[
                (coarse_row + half) * SENT : (coarse_row + half + 1) * SENT, split:
            ]

    @pl.when(even)
    def _():
        fill(first, 1, 2)
        fill(second, 0, 0)

    @pl.when(jnp.logical_not(even))
    def _():
        fill(first, 0, 0)
        fill(second, 1, 2)


def spread_out(target, row, rows, width, even, odd):
    count = rows * SLOT
    here = slice(row * SLOT, row * SLOT + count)
    target[here, :width] = pltpu.roll(odd, 1, 0).astype(BF16)
    target[here, width : 2 * width] = even.astype(BF16)
    target[here, 2 * width : 3 * width] = odd.astype(BF16)
    target[here, 3 * width :] = pltpu.roll(even, count - 1, 0).astype(BF16)


def unite_kernel(blocks, *refs):
    (block, first, second, lift_w, lift_b, merge_w, out_w, out_b) = refs[:8]
    (inner1_w, inner1_b, outer1_w, outer1_b, inner2_w, inner2_b, outer2_w, outer2_b) = refs[8:16]
    outs = refs[16 : 16 + QUAD]
    (lift_v, out_v, merge_v, inner1_v, outer1_v, inner2_v, outer2_v) = refs[20:27]
    (window, coarse, thin, mask, wide_x, x_a, x_b, kept_r, kept_m, fine) = refs[27:37]
    sems = refs[37]
    own, number = place()
    split = window.shape[1]
    width = x_a.shape[1] // 4

    copies = [
        pltpu.make_async_copy(source, target, sems.at[i])
        for i, (source, target) in enumerate(
            (
                (lift_w, lift_v),
                (merge_w, merge_v),
                (out_w, out_v),
                (inner1_w, inner1_v),
                (outer1_w, outer1_v),
                (inner2_w, inner2_v),
                (outer2_w, outer2_v),
            )
        )
    ]
    for copy in copies:
        copy.start()

    rows_w = mask.shape[0] // SLOT
    lane = lax.broadcasted_iota(jnp.int32, (SLOT, 128), 0)
    token = lane + (own * SEG - HALO)
    inside = (token >= 0) & (token < GW) & (lane < SEG + 2 * HALO)
    inside = jnp.where(inside, 1.0, 0.0)
    for r in range(rows_w):
        at = number * (2 * QUAD) + (r - 5)
        good = jnp.where((at >= 0) & (at < blocks * 2 * QUAD), 1.0, 0.0)
        mask[r * SLOT : (r + 1) * SLOT] = inside * good

    def masked(value, row, rows):
        keep = mask[row * SLOT : (row + rows) * SLOT]
        keep = jnp.concatenate([keep] * (value.shape[1] // 128), axis=1)
        return jnp.where(keep > 0.5, value, 0.0)

    tail = SLOT - SENT
    for i in range(QUAD + 2 * HALO):
        window[i * SLOT + SENT : (i + 1) * SLOT] = jnp.zeros((tail, split), BF16)
    for i in range(QUAD + 4):
        coarse[i * SLOT + SENT : (i + 1) * SLOT] = jnp.zeros((tail, width), BF16)
    for i in range(QUAD):
        there = slice(i * SENT, (i + 1) * SENT)
        at = (i + HALO) * SLOT
        window[at : at + SENT] = block[there, :split]
        at = (i + 2) * SLOT
        coarse[at : at + SENT] = block[there, split:]

    def land(payload, row, coarse_row):
        for i in range(HALO):
            at = (row + i) * SLOT
            window[at : at + SENT] = payload[i * SENT : (i + 1) * SENT]
        for half in range(2):
            at = (coarse_row + half) * SLOT
            coarse[at : at + SENT] = payload[HALO * SENT :, half * width : (half + 1) * width]

    even_block = lax.rem(number, 2) == 0

    @pl.when(even_block)
    def _():
        land(second, 0, 0)
        land(first, QUAD + HALO, QUAD + 2)

    @pl.when(jnp.logical_not(even_block))
    def _():
        land(first, 0, 0)
        land(second, QUAD + HALO, QUAD + 2)

    @pl.when(number == 0)
    def _():
        coarse[SLOT : SLOT + SENT] = block[:SENT, split:]

    @pl.when(number == blocks - 1)
    def _():
        at = (QUAD + 2) * SLOT
        coarse[at : at + SENT] = block[(QUAD - 1) * SENT :, split:]

    copies[0].wait()
    tall = rows_w // 2
    for a in range(2):
        lhs = window[(1 - a) * SLOT : (1 - a + tall) * SLOT]
        for b in range(2):
            lifted = jnp.dot(
                lhs,
                lift_v[:, (2 * a + b) * split : (2 * a + b + 1) * split],
                preferred_element_type=F32,
            )
            for i in range(tall):
                row = 2 * i + (1 - a)
                value = masked(lifted[i * SLOT : (i + 1) * SLOT] + lift_b[...], row, 1)
                here = slice(row * SLOT, (row + 1) * SLOT)
                plain, moved = (1, 3) if b == 0 else (2, 0)
                shift = SLOT - 1 if b == 0 else 1
                wide_x[here, plain * split : (plain + 1) * split] = value.astype(BF16)
                wide_x[here, moved * split : (moved + 1) * split] = pltpu.roll(
                    value, shift, 0
                ).astype(BF16)

    def conv(source, weight, channels, row, rows):
        total = None
        for dy in range(3):
            piece = source[(row + dy) * SLOT : (row + dy + rows) * SLOT]
            lhs = jnp.concatenate([piece[:, : 3 * channels], piece[:, channels:]], axis=0)
            part = jnp.dot(
                lhs,
                weight[3 * dy * channels : 3 * (dy + 1) * channels],
                preferred_element_type=F32,
            )
            total = part if total is None else total + part
        return total[: rows * SLOT], total[rows * SLOT :]

    def chunks(rows, size):
        return [(row, min(size, rows - row)) for row in range(0, rows, size)]

    copies[1].wait()
    for row, rows in chunks(rows_w - 2, 4):
        even, odd = conv(wide_x, merge_v, split, row, rows)
        here = slice(row * SLOT, (row + rows) * SLOT)
        kept_r[0, here] = even.astype(BF16)
        kept_r[1, here] = odd.astype(BF16)
        even = masked(jnp.maximum(even, 0.0), row + 1, rows)
        odd = masked(jnp.maximum(odd, 0.0), row + 1, rows)
        spread_out(x_a, row, rows, width, even, odd)

    copies[2].wait()
    thin[...] = jnp.dot(coarse[...], out_v[...], preferred_element_type=F32)

    copies[3].wait()
    for row, rows in chunks(rows_w - 4, 7):
        even, odd = conv(x_a, inner1_v, width, row, rows)
        even = masked(jnp.maximum(even + inner1_b[...], 0.0), row + 2, rows)
        odd = masked(jnp.maximum(odd + inner1_b[...], 0.0), row + 2, rows)
        spread_out(x_b, row, rows, width, even, odd)

    copies[4].wait()
    bias = outer1_b[...] + out_b[...]
    for row, rows in chunks(rows_w - 6, 4):
        even, odd = conv(x_b, outer1_v, width, row, rows)
        left, right = [], []
        for r in range(row, row + rows):
            i, a = divmod(r + 2, 2)
            near = thin[i * SLOT : (i + 1) * SLOT]
            far = i - 1 if a == 0 else i + 1
            band = 0.75 * near + 0.25 * thin[far * SLOT : (far + 1) * SLOT]
            left.append(0.25 * pltpu.roll(band, 1, 0) + 0.75 * band)
            right.append(0.75 * band + 0.25 * pltpu.roll(band, SLOT - 1, 0))
        old = slice((row + 2) * SLOT, (row + 2 + rows) * SLOT)
        even = even + bias + kept_r[0, old].astype(F32) + jnp.concatenate(left, axis=0)
        odd = odd + bias + kept_r[1, old].astype(F32) + jnp.concatenate(right, axis=0)
        here = slice(row * SLOT, (row + rows) * SLOT)
        kept_m[0, here] = even.astype(BF16)
        kept_m[1, here] = odd.astype(BF16)
        even = masked(jnp.maximum(even, 0.0), row + 3, rows)
        odd = masked(jnp.maximum(odd, 0.0), row + 3, rows)
        spread_out(x_a, row, rows, width, even, odd)

    copies[5].wait()
    for row, rows in chunks(rows_w - 8, 5):
        even, odd = conv(x_a, inner2_v, width, row, rows)
        even = masked(jnp.maximum(even + inner2_b[...], 0.0), row + 4, rows)
        odd = masked(jnp.maximum(odd + inner2_b[...], 0.0), row + 4, rows)
        spread_out(x_b, row, rows, width, even, odd)

    copies[6].wait()
    for row, rows in chunks(rows_w - 10, 4):
        pair = conv(x_b, outer2_v, width, row, rows)
        for parity in range(2):
            old = slice((row + 2) * SLOT, (row + 2 + rows) * SLOT)
            value = pair[parity] + outer2_b[...] + kept_m[parity, old].astype(F32)
            for r in range(rows):
                cells = value[r * SLOT + HALO : r * SLOT + HALO + SEG]
                base = (row + r) * 2 * SEG + parity
                for half in range(width // 128):
                    fine[half, pl.ds(base, SEG, 2), :] = cells[:, half * 128 : (half + 1) * 128]
    for k in range(QUAD):
        start = pl.multiple_of(lax.bitwise_xor(own, k) * (4 * SEG), 16)
        for half in range(width // 128):
            outs[k][:, half * 128 : (half + 1) * 128] = fine[half, pl.ds(start, 4 * SEG), :].astype(
                BF16
            )


def assemble_kernel(*refs):
    pieces, out = refs[:QUAD], refs[QUAD]
    own, _ = place()
    for k in range(QUAD):
        start = pl.multiple_of(lax.bitwise_xor(own, k) * (2 * SEG), 16)
        for r in range(2):
            out[r, pl.ds(start, 2 * SEG), :] = pieces[k][r * 2 * SEG : (r + 1) * 2 * SEG]


def body(
    tap_two,
    coarse_path,
    proj_weight,
    proj_bias,
    lift_weight,
    lift_bias,
    merge_weight,
    out_weight,
    out_bias,
    first_inner_w,
    first_inner_b,
    first_outer_w,
    first_outer_b,
    second_inner_w,
    second_inner_b,
    second_outer_w,
    second_outer_b,
):
    count = lax.axis_size("rows")
    if tap_two.shape[0] != GW or count % QUAD:
        raise ValueError("unsupported split")
    blocks = count // QUAD
    split = proj_weight.shape[1]
    width = out_weight.shape[1]
    shape = jax.ShapeDtypeStruct

    def swap(value, k):
        return lax.ppermute(value, "rows", [(i, i ^ k) for i in range(count)])

    def between(value, parity):
        pairs = []
        for low in range(parity, blocks - 1, 2):
            for q in range(QUAD):
                a, b = low * QUAD + q, (low + 1) * QUAD + q
                pairs += [(a, b), (b, a)]
        return lax.ppermute(value, "rows", pairs)

    segments = pl.pallas_call(
        project_kernel,
        out_shape=[shape((SENT, split + width), BF16)] * QUAD,
        in_specs=[VMEM] * 4,
        out_specs=[VMEM] * QUAD,
        scratch_shapes=[pltpu.VMEM((GW + 16, split), F32), pltpu.VMEM((GW + 16, width), F32)],
    )(tap_two, coarse_path, proj_weight, proj_bias[None])
    segments = [segments[0]] + [swap(segments[k], k) for k in range(1, QUAD)]
    block, first, second = pl.pallas_call(
        functools.partial(pack_kernel, split),
        out_shape=[shape((QUAD * SENT, split + width), BF16)]
        + [shape(((HALO + 1) * SENT, split), BF16)] * 2,
        in_specs=[VMEM] * QUAD,
        out_specs=[VMEM] * 3,
    )(*segments)
    first, second = between(first, 0), between(second, 1)

    rows_w = 2 * QUAD + 10
    weights = (
        lift_weight,
        out_weight,
        merge_weight,
        first_inner_w,
        first_outer_w,
        second_inner_w,
        second_outer_w,
    )
    flops = 2 * rows_w * SLOT * (2 * split * split + 4 * 9 * split * width)
    outs = pl.pallas_call(
        functools.partial(unite_kernel, blocks),
        out_shape=[shape((4 * SEG, width), BF16)] * QUAD,
        in_specs=[VMEM] * 3
        + [ANY, VMEM, ANY, ANY, VMEM, ANY, VMEM, ANY, VMEM, ANY, VMEM, ANY, VMEM],
        out_specs=[VMEM] * QUAD,
        scratch_shapes=[pltpu.VMEM(w.shape, BF16) for w in weights]
        + [
            pltpu.VMEM(((QUAD + 2 * HALO) * SLOT, split), BF16),
            pltpu.VMEM(((QUAD + 4) * SLOT, width), BF16),
            pltpu.VMEM(((QUAD + 4) * SLOT, width), F32),
            pltpu.VMEM((rows_w * SLOT, 128), F32),
            pltpu.VMEM((rows_w * SLOT, 4 * split), BF16),
            pltpu.VMEM(((rows_w - 2) * SLOT, 4 * width), BF16),
            pltpu.VMEM(((rows_w - 4) * SLOT, 4 * width), BF16),
            pltpu.VMEM((2, (rows_w - 2) * SLOT, width), BF16),
            pltpu.VMEM((2, (rows_w - 6) * SLOT, width), BF16),
            pltpu.VMEM((width // 128, 4 * QUAD * SEG, 128), F32),
            pltpu.SemaphoreType.DMA((7,)),
        ],
        compiler_params=pltpu.CompilerParams(vmem_limit_bytes=60 * 1024 * 1024),
        cost_estimate=pl.CostEstimate(flops=flops, bytes_accessed=10_000_000, transcendentals=0),
    )(
        block,
        first,
        second,
        lift_weight,
        lift_bias[None],
        merge_weight,
        out_weight,
        out_bias[None],
        first_inner_w,
        first_inner_b[None],
        first_outer_w,
        first_outer_b[None],
        second_inner_w,
        second_inner_b[None],
        second_outer_w,
        second_outer_b[None],
    )
    pieces = [outs[0]] + [swap(outs[k], k) for k in range(1, QUAD)]
    return pl.pallas_call(
        assemble_kernel,
        out_shape=shape((2, 2 * GW, width), BF16),
        in_specs=[VMEM] * QUAD,
        out_specs=VMEM,
    )(*pieces)


def solution(mesh):
    return jax.shard_map(
        body,
        mesh=mesh,
        in_specs=(P(("groups", "rows"), None), P(("groups", "rows"), None)) + (P(),) * 15,
        out_specs=P(("groups", "rows"), None, None),
        check_vma=False,
    )
```

```python
import functools

import jax
import jax.numpy as jnp
from jax import lax
from jax.experimental import pallas as pl
from jax.experimental.pallas import tpu as pltpu
from jax.sharding import PartitionSpec as P

GW = 192
QUAD = 4
SEG = GW // QUAD
HALO = 3
SENT = 56
SLOT = 64

BF16, F32 = jnp.bfloat16, jnp.float32
MIB = 1024 * 1024
VMEM = pl.BlockSpec(memory_space=pltpu.VMEM)
HBM = pl.BlockSpec(memory_space=pltpu.HBM)


def place():
    position = lax.axis_index("rows")
    return lax.rem(position, QUAD), lax.div(position, QUAD)


def project_kernel(tap_hbm, coarse_hbm, weight_hbm, bias_hbm, *rest):
    segments, (grid, sparse, tap, coarse, weight, bias, sems) = rest[:QUAD], rest[QUAD:]
    own, _ = place()
    copies = [
        pltpu.make_async_copy(source, target, sems.at[i])
        for i, (source, target) in enumerate(
            ((weight_hbm, weight), (tap_hbm, tap), (coarse_hbm, coarse), (bias_hbm, bias))
        )
    ]
    for copy in copies:
        copy.start()
    edge = grid.shape[0] - GW
    grid[0:8] = jnp.zeros((8, grid.shape[1]), F32)
    grid[GW:] = jnp.zeros((edge, grid.shape[1]), F32)
    copies[0].wait()
    copies[1].wait()
    copies[3].wait()
    grid[HALO : HALO + GW] = jnp.dot(tap[...], weight[...], preferred_element_type=F32) + bias[...]
    copies[2].wait()
    wide = coarse[...].astype(F32)
    sparse[0:8] = jnp.zeros((8, sparse.shape[1]), F32)
    sparse[GW:] = jnp.zeros((edge, sparse.shape[1]), F32)
    sparse[HALO : HALO + GW] = wide
    sparse[HALO - 1 : HALO] = wide[:1]
    sparse[HALO + GW : HALO + GW + 1] = wide[GW - 1 :]
    split = grid.shape[1]
    for k in range(QUAD):
        start = pl.multiple_of(lax.bitwise_xor(own, k) * SEG, 16)
        segments[k][:, :split] = grid[pl.ds(start, SENT), :].astype(BF16)
        segments[k][:, split:] = sparse[pl.ds(start, SENT), :].astype(BF16)


def pack_kernel(split, *refs):
    segments, (block, first, second) = refs[:QUAD], refs[QUAD:]
    own, number = place()
    for row in range(QUAD):
        for k in range(QUAD):

            @pl.when(own == row ^ k)
            def _():
                block[row * SENT : (row + 1) * SENT] = segments[k][...]

    coarse = block.shape[1] - split
    even = lax.rem(number, 2) == 0

    def fill(payload, row, coarse_row):
        payload[: HALO * SENT] = block[row * SENT : (row + HALO) * SENT, :split]
        for half in range(2):
            payload[HALO * SENT :, half * coarse : (half + 1) * coarse] = block[
                (coarse_row + half) * SENT : (coarse_row + half + 1) * SENT, split:
            ]

    @pl.when(even)
    def _():
        fill(first, 1, 2)
        fill(second, 0, 0)

    @pl.when(jnp.logical_not(even))
    def _():
        fill(first, 0, 0)
        fill(second, 1, 2)


def spread_out(target, row, rows, width, even, odd):
    count = rows * SLOT
    here = slice(row * SLOT, row * SLOT + count)
    target[here, :width] = pltpu.roll(odd, 1, 0).astype(BF16)
    target[here, width : 2 * width] = even.astype(BF16)
    target[here, 2 * width : 3 * width] = odd.astype(BF16)
    target[here, 3 * width :] = pltpu.roll(even, count - 1, 0).astype(BF16)


def unite_kernel(blocks, *refs):
    (block, first, second, lift_w, lift_b, merge_w, out_w, out_b) = refs[:8]
    (inner1_w, inner1_b, outer1_w, outer1_b, inner2_w, inner2_b, outer2_w, outer2_b) = refs[8:16]
    outs = refs[16 : 16 + QUAD]
    (lift_v, out_v, merge_v, inner1_v, outer1_v, inner2_v, outer2_v) = refs[20:27]
    (window, coarse, thin, mask, wide_x, x_a, x_b, kept_r, kept_m, fine) = refs[27:37]
    sems = refs[37]
    own, number = place()
    split = window.shape[1]
    width = x_a.shape[1] // 4

    copies = [
        pltpu.make_async_copy(source, target, sems.at[i])
        for i, (source, target) in enumerate(
            (
                (lift_w, lift_v),
                (merge_w, merge_v),
                (out_w, out_v),
                (inner1_w, inner1_v),
                (outer1_w, outer1_v),
                (inner2_w, inner2_v),
                (outer2_w, outer2_v),
            )
        )
    ]
    for copy in copies:
        copy.start()

    rows_w = mask.shape[0] // SLOT
    lane = lax.broadcasted_iota(jnp.int32, (SLOT, 128), 0)
    token = lane + (own * SEG - HALO)
    inside = (token >= 0) & (token < GW) & (lane < SEG + 2 * HALO)
    inside = jnp.where(inside, 1.0, 0.0)
    for r in range(rows_w):
        at = number * (2 * QUAD) + (r - 5)
        good = jnp.where((at >= 0) & (at < blocks * 2 * QUAD), 1.0, 0.0)
        mask[r * SLOT : (r + 1) * SLOT] = inside * good

    def masked(value, row, rows):
        keep = mask[row * SLOT : (row + rows) * SLOT]
        keep = jnp.concatenate([keep] * (value.shape[1] // 128), axis=1)
        return jnp.where(keep > 0.5, value, 0.0)

    tail = SLOT - SENT
    for i in range(QUAD + 2 * HALO):
        window[i * SLOT + SENT : (i + 1) * SLOT] = jnp.zeros((tail, split), BF16)
    for i in range(QUAD + 4):
        coarse[i * SLOT + SENT : (i + 1) * SLOT] = jnp.zeros((tail, width), BF16)
    for i in range(QUAD):
        there = slice(i * SENT, (i + 1) * SENT)
        at = (i + HALO) * SLOT
        window[at : at + SENT] = block[there, :split]
        at = (i + 2) * SLOT
        coarse[at : at + SENT] = block[there, split:]

    def land(payload, row, coarse_row):
        for i in range(HALO):
            at = (row + i) * SLOT
            window[at : at + SENT] = payload[i * SENT : (i + 1) * SENT]
        for half in range(2):
            at = (coarse_row + half) * SLOT
            coarse[at : at + SENT] = payload[HALO * SENT :, half * width : (half + 1) * width]

    even_block = lax.rem(number, 2) == 0

    @pl.when(even_block)
    def _():
        land(second, 0, 0)
        land(first, QUAD + HALO, QUAD + 2)

    @pl.when(jnp.logical_not(even_block))
    def _():
        land(first, 0, 0)
        land(second, QUAD + HALO, QUAD + 2)

    @pl.when(number == 0)
    def _():
        coarse[SLOT : SLOT + SENT] = block[:SENT, split:]

    @pl.when(number == blocks - 1)
    def _():
        at = (QUAD + 2) * SLOT
        coarse[at : at + SENT] = block[(QUAD - 1) * SENT :, split:]

    copies[0].wait()
    tall = rows_w // 2
    for a in range(2):
        lhs = window[(1 - a) * SLOT : (1 - a + tall) * SLOT]
        for b in range(2):
            lifted = jnp.dot(
                lhs,
                lift_v[:, (2 * a + b) * split : (2 * a + b + 1) * split],
                preferred_element_type=F32,
            )
            for i in range(tall):
                row = 2 * i + (1 - a)
                value = masked(lifted[i * SLOT : (i + 1) * SLOT] + lift_b[...], row, 1)
                here = slice(row * SLOT, (row + 1) * SLOT)
                plain, moved = (1, 3) if b == 0 else (2, 0)
                shift = SLOT - 1 if b == 0 else 1
                wide_x[here, plain * split : (plain + 1) * split] = value.astype(BF16)
                wide_x[here, moved * split : (moved + 1) * split] = pltpu.roll(
                    value, shift, 0
                ).astype(BF16)

    def conv(source, weight, channels, row, rows):
        total = None
        for dy in range(3):
            piece = source[(row + dy) * SLOT : (row + dy + rows) * SLOT]
            lhs = jnp.concatenate([piece[:, : 3 * channels], piece[:, channels:]], axis=0)
            part = jnp.dot(
                lhs,
                weight[3 * dy * channels : 3 * (dy + 1) * channels],
                preferred_element_type=F32,
            )
            total = part if total is None else total + part
        return total[: rows * SLOT], total[rows * SLOT :]

    def chunks(rows, size):
        return [(row, min(size, rows - row)) for row in range(0, rows, size)]

    copies[1].wait()
    for row, rows in chunks(rows_w - 2, 4):
        even, odd = conv(wide_x, merge_v, split, row, rows)
        here = slice(row * SLOT, (row + rows) * SLOT)
        kept_r[0, here] = even.astype(BF16)
        kept_r[1, here] = odd.astype(BF16)
        even = masked(jnp.maximum(even, 0.0), row + 1, rows)
        odd = masked(jnp.maximum(odd, 0.0), row + 1, rows)
        spread_out(x_a, row, rows, width, even, odd)

    copies[2].wait()
    thin[...] = jnp.dot(coarse[...], out_v[...], preferred_element_type=F32)

    copies[3].wait()
    for row, rows in chunks(rows_w - 4, 7):
        even, odd = conv(x_a, inner1_v, width, row, rows)
        even = masked(jnp.maximum(even + inner1_b[...], 0.0), row + 2, rows)
        odd = masked(jnp.maximum(odd + inner1_b[...], 0.0), row + 2, rows)
        spread_out(x_b, row, rows, width, even, odd)

    copies[4].wait()
    bias = outer1_b[...] + out_b[...]
    for row, rows in chunks(rows_w - 6, 4):
        even, odd = conv(x_b, outer1_v, width, row, rows)
        left, right = [], []
        for r in range(row, row + rows):
            i, a = divmod(r + 2, 2)
            near = thin[i * SLOT : (i + 1) * SLOT]
            far = i - 1 if a == 0 else i + 1
            band = 0.75 * near + 0.25 * thin[far * SLOT : (far + 1) * SLOT]
            left.append(0.25 * pltpu.roll(band, 1, 0) + 0.75 * band)
            right.append(0.75 * band + 0.25 * pltpu.roll(band, SLOT - 1, 0))
        old = slice((row + 2) * SLOT, (row + 2 + rows) * SLOT)
        even = even + bias + kept_r[0, old].astype(F32) + jnp.concatenate(left, axis=0)
        odd = odd + bias + kept_r[1, old].astype(F32) + jnp.concatenate(right, axis=0)
        here = slice(row * SLOT, (row + rows) * SLOT)
        kept_m[0, here] = even.astype(BF16)
        kept_m[1, here] = odd.astype(BF16)
        even = masked(jnp.maximum(even, 0.0), row + 3, rows)
        odd = masked(jnp.maximum(odd, 0.0), row + 3, rows)
        spread_out(x_a, row, rows, width, even, odd)

    copies[5].wait()
    for row, rows in chunks(rows_w - 8, 5):
        even, odd = conv(x_a, inner2_v, width, row, rows)
        even = masked(jnp.maximum(even + inner2_b[...], 0.0), row + 4, rows)
        odd = masked(jnp.maximum(odd + inner2_b[...], 0.0), row + 4, rows)
        spread_out(x_b, row, rows, width, even, odd)

    copies[6].wait()
    for row, rows in chunks(rows_w - 10, 4):
        pair = conv(x_b, outer2_v, width, row, rows)
        for parity in range(2):
            old = slice((row + 2) * SLOT, (row + 2 + rows) * SLOT)
            value = pair[parity] + outer2_b[...] + kept_m[parity, old].astype(F32)
            for r in range(rows):
                cells = value[r * SLOT + HALO : r * SLOT + HALO + SEG]
                base = (row + r) * 2 * SEG + parity
                for half in range(width // 128):
                    fine[half, pl.ds(base, SEG, 2), :] = cells[:, half * 128 : (half + 1) * 128]
    for k in range(QUAD):
        start = pl.multiple_of(lax.bitwise_xor(own, k) * (4 * SEG), 16)
        for half in range(width // 128):
            outs[k][:, half * 128 : (half + 1) * 128] = fine[half, pl.ds(start, 4 * SEG), :].astype(
                BF16
            )


def assemble_kernel(*refs):
    pieces, out = refs[:QUAD], refs[QUAD]
    own, _ = place()
    for k in range(QUAD):
        start = pl.multiple_of(lax.bitwise_xor(own, k) * (2 * SEG), 16)
        for r in range(2):
            out[r, pl.ds(start, 2 * SEG), :] = pieces[k][r * 2 * SEG : (r + 1) * 2 * SEG]


def body(
    tap_two,
    coarse_path,
    proj_weight,
    proj_bias,
    lift_weight,
    lift_bias,
    merge_weight,
    out_weight,
    out_bias,
    first_inner_w,
    first_inner_b,
    first_outer_w,
    first_outer_b,
    second_inner_w,
    second_inner_b,
    second_outer_w,
    second_outer_b,
):
    count = lax.axis_size("rows")
    if tap_two.shape[0] != GW or count % QUAD:
        raise ValueError("unsupported split")
    blocks = count // QUAD
    split = proj_weight.shape[1]
    width = out_weight.shape[1]
    shape = jax.ShapeDtypeStruct
    hbm = functools.partial(pltpu.with_memory_space_constraint, memory_space=pltpu.HBM)

    def swap(value, k):
        return lax.ppermute(value, "rows", [(i, i ^ k) for i in range(count)])

    def between(value, parity):
        pairs = []
        for low in range(parity, blocks - 1, 2):
            for q in range(QUAD):
                a, b = low * QUAD + q, (low + 1) * QUAD + q
                pairs += [(a, b), (b, a)]
        return lax.ppermute(value, "rows", pairs)

    segments = pl.pallas_call(
        project_kernel,
        out_shape=[shape((SENT, split + width), BF16)] * QUAD,
        in_specs=[HBM] * 4,
        out_specs=[VMEM] * QUAD,
        scratch_shapes=[
            pltpu.VMEM((GW + 16, split), F32),
            pltpu.VMEM((GW + 16, width), F32),
            pltpu.VMEM(tap_two.shape, BF16),
            pltpu.VMEM(coarse_path.shape, BF16),
            pltpu.VMEM(proj_weight.shape, BF16),
            pltpu.VMEM((1, split), F32),
            pltpu.SemaphoreType.DMA((4,)),
        ],
        compiler_params=pltpu.CompilerParams(vmem_limit_bytes=8 * MIB),
    )(hbm(tap_two), hbm(coarse_path), hbm(proj_weight), hbm(proj_bias[None]))
    segments = [segments[0]] + [swap(segments[k], k) for k in range(1, QUAD)]
    block, first, second = pl.pallas_call(
        functools.partial(pack_kernel, split),
        out_shape=[shape((QUAD * SENT, split + width), BF16)]
        + [shape(((HALO + 1) * SENT, split), BF16)] * 2,
        in_specs=[VMEM] * QUAD,
        out_specs=[VMEM] * 3,
        compiler_params=pltpu.CompilerParams(vmem_limit_bytes=4 * MIB),
    )(*segments)
    first, second = between(first, 0), between(second, 1)

    rows_w = 2 * QUAD + 10
    weights = (
        lift_weight,
        out_weight,
        merge_weight,
        first_inner_w,
        first_outer_w,
        second_inner_w,
        second_outer_w,
    )
    flops = 2 * rows_w * SLOT * (2 * split * split + 4 * 9 * split * width)
    outs = pl.pallas_call(
        functools.partial(unite_kernel, blocks),
        out_shape=[shape((4 * SEG, width), BF16)] * QUAD,
        in_specs=[VMEM] * 3
        + [HBM, VMEM, HBM, HBM, VMEM, HBM, VMEM, HBM, VMEM, HBM, VMEM, HBM, VMEM],
        out_specs=[VMEM] * QUAD,
        scratch_shapes=[pltpu.VMEM(w.shape, BF16) for w in weights]
        + [
            pltpu.VMEM(((QUAD + 2 * HALO) * SLOT, split), BF16),
            pltpu.VMEM(((QUAD + 4) * SLOT, width), BF16),
            pltpu.VMEM(((QUAD + 4) * SLOT, width), F32),
            pltpu.VMEM((rows_w * SLOT, 128), F32),
            pltpu.VMEM((rows_w * SLOT, 4 * split), BF16),
            pltpu.VMEM(((rows_w - 2) * SLOT, 4 * width), BF16),
            pltpu.VMEM(((rows_w - 4) * SLOT, 4 * width), BF16),
            pltpu.VMEM((2, (rows_w - 2) * SLOT, width), BF16),
            pltpu.VMEM((2, (rows_w - 6) * SLOT, width), BF16),
            pltpu.VMEM((width // 128, 4 * QUAD * SEG, 128), F32),
            pltpu.SemaphoreType.DMA((7,)),
        ],
        compiler_params=pltpu.CompilerParams(vmem_limit_bytes=32 * MIB),
        cost_estimate=pl.CostEstimate(flops=flops, bytes_accessed=10_000_000, transcendentals=0),
    )(
        block,
        first,
        second,
        hbm(lift_weight),
        lift_bias[None],
        hbm(merge_weight),
        hbm(out_weight),
        out_bias[None],
        hbm(first_inner_w),
        first_inner_b[None],
        hbm(first_outer_w),
        first_outer_b[None],
        hbm(second_inner_w),
        second_inner_b[None],
        hbm(second_outer_w),
        second_outer_b[None],
    )
    pieces = [outs[0]] + [swap(outs[k], k) for k in range(1, QUAD)]
    return pl.pallas_call(
        assemble_kernel,
        out_shape=shape((2, 2 * GW, width), BF16),
        in_specs=[VMEM] * QUAD,
        out_specs=VMEM,
        compiler_params=pltpu.CompilerParams(vmem_limit_bytes=4 * MIB),
    )(*pieces)


def solution(mesh):
    return jax.shard_map(
        body,
        mesh=mesh,
        in_specs=(P(("groups", "rows"), None), P(("groups", "rows"), None)) + (P(),) * 15,
        out_specs=P(("groups", "rows"), None, None),
        check_vma=False,
    )
```

```python
import functools

import jax
import jax.numpy as jnp
from jax import lax
from jax.experimental import pallas as pl
from jax.experimental.pallas import tpu as pltpu
from jax.sharding import PartitionSpec as P

GW = 192
QUAD = 4
SEG = GW // QUAD
HALO = 3
SENT = 56
SLOT = 64

BF16, F32 = jnp.bfloat16, jnp.float32
MIB = 1024 * 1024
VMEM = pl.BlockSpec(memory_space=pltpu.VMEM)
HBM = pl.BlockSpec(memory_space=pltpu.HBM)


def place():
    position = lax.axis_index("rows")
    return lax.rem(position, QUAD), lax.div(position, QUAD)


def project_kernel(tap_hbm, coarse_hbm, weight_hbm, bias_hbm, *rest):
    segments, (grid, sparse, tap, coarse, weight, bias, sems) = rest[:QUAD], rest[QUAD:]
    own, _ = place()
    copies = [
        pltpu.make_async_copy(source, target, sems.at[i])
        for i, (source, target) in enumerate(
            ((weight_hbm, weight), (tap_hbm, tap), (coarse_hbm, coarse), (bias_hbm, bias))
        )
    ]
    for copy in copies:
        copy.start()
    edge = grid.shape[0] - GW
    grid[0:8] = jnp.zeros((8, grid.shape[1]), F32)
    grid[GW:] = jnp.zeros((edge, grid.shape[1]), F32)
    copies[0].wait()
    copies[1].wait()
    copies[3].wait()
    grid[HALO : HALO + GW] = jnp.dot(tap[...], weight[...], preferred_element_type=F32) + bias[...]
    copies[2].wait()
    wide = coarse[...].astype(F32)
    sparse[0:8] = jnp.zeros((8, sparse.shape[1]), F32)
    sparse[GW:] = jnp.zeros((edge, sparse.shape[1]), F32)
    sparse[HALO : HALO + GW] = wide
    sparse[HALO - 1 : HALO] = wide[:1]
    sparse[HALO + GW : HALO + GW + 1] = wide[GW - 1 :]
    split = grid.shape[1]
    for k in range(QUAD):
        start = pl.multiple_of(lax.bitwise_xor(own, k) * SEG, 16)
        segments[k][:, :split] = grid[pl.ds(start, SENT), :].astype(BF16)
        segments[k][:, split:] = sparse[pl.ds(start, SENT), :].astype(BF16)


def pack_kernel(split, *refs):
    segments, (block, first, second) = refs[:QUAD], refs[QUAD:]
    own, number = place()
    for row in range(QUAD):
        for k in range(QUAD):

            @pl.when(own == row ^ k)
            def _():
                block[row * SENT : (row + 1) * SENT] = segments[k][...]

    coarse = block.shape[1] - split
    even = lax.rem(number, 2) == 0

    def fill(payload, row, coarse_row):
        payload[: HALO * SENT] = block[row * SENT : (row + HALO) * SENT, :split]
        for half in range(2):
            payload[HALO * SENT :, half * coarse : (half + 1) * coarse] = block[
                (coarse_row + half) * SENT : (coarse_row + half + 1) * SENT, split:
            ]

    @pl.when(even)
    def _():
        fill(first, 1, 2)
        fill(second, 0, 0)

    @pl.when(jnp.logical_not(even))
    def _():
        fill(first, 0, 0)
        fill(second, 1, 2)


def rows_at(row, rows):
    if isinstance(row, int):
        return pl.ds(row * SLOT, rows * SLOT)
    return pl.ds(pl.multiple_of(row * SLOT, SLOT), rows * SLOT)


def masked(mask, value, row, rows):
    keep = mask[rows_at(row, rows)]
    keep = jnp.concatenate([keep] * (value.shape[1] // 128), axis=1)
    return jnp.where(keep > 0.5, value, 0.0)


def spread_out(target, row, rows, even, odd):
    here, count, width = rows_at(row, rows), rows * SLOT, even.shape[1]
    target[here, :width] = pltpu.roll(odd, 1, 0).astype(BF16)
    target[here, width : 2 * width] = even.astype(BF16)
    target[here, 2 * width : 3 * width] = odd.astype(BF16)
    target[here, 3 * width :] = pltpu.roll(even, count - 1, 0).astype(BF16)


def conv(source, weight, pieces):
    channels = source.shape[1] // 4
    total = None
    for dy in range(3):
        parts = []
        for row, rows in pieces:
            piece = source[rows_at(row + dy, rows)]
            parts += [piece[:, : 3 * channels], piece[:, channels:]]
        part = jnp.dot(
            jnp.concatenate(parts, axis=0),
            weight[3 * dy * channels : 3 * (dy + 1) * channels],
            preferred_element_type=F32,
        )
        total = part if total is None else total + part
    results, at = [], 0
    for _, rows in pieces:
        count = rows * SLOT
        results.append((total[at : at + count], total[at + count : at + 2 * count]))
        at += 2 * count
    return results


def lift(window, weight, bias, mask, target, tokens):
    split = window.shape[1]
    for a in range(2):
        first, lines = tokens[a]
        lhs = window[first * SLOT : (first + len(lines)) * SLOT]
        for b in range(2):
            lifted = jnp.dot(
                lhs,
                weight[:, (2 * a + b) * split : (2 * a + b + 1) * split],
                preferred_element_type=F32,
            )
            plain, moved, shift = (1, 3, SLOT - 1) if b == 0 else (2, 0, 1)
            for i, row in enumerate(lines):
                value = masked(mask, lifted[i * SLOT : (i + 1) * SLOT] + bias[...], row, 1)
                here = rows_at(row, 1)
                target[here, plain * split : (plain + 1) * split] = value.astype(BF16)
                value = pltpu.roll(value, shift, 0).astype(BF16)
                target[here, moved * split : (moved + 1) * split] = value


def enlarged(thin, first, row):
    i, a = divmod(row, 2)
    far = i - 1 if a == 0 else i + 1
    i, far = i - first, far - first
    band = 0.75 * thin[i * SLOT : (i + 1) * SLOT] + 0.25 * thin[far * SLOT : (far + 1) * SLOT]
    left = 0.25 * pltpu.roll(band, 1, 0) + 0.75 * band
    right = 0.75 * band + 0.25 * pltpu.roll(band, SLOT - 1, 0)
    return left, right


def make_reassembled(state, pieces):
    for (row, rows), pair in zip(pieces, conv(state.wide, state.merge_w, pieces), strict=True):
        for parity in range(2):
            state.kept_r[parity, rows_at(row, rows)] = pair[parity].astype(BF16)
        pair = [masked(state.mask, jnp.maximum(v, 0.0), row + 1, rows) for v in pair]
        spread_out(state.x_r, row, rows, *pair)


def make_inner(source, weight, bias, mask, target, offset, pieces):
    for (row, rows), pair in zip(pieces, conv(source, weight, pieces), strict=True):
        pair = [masked(mask, jnp.maximum(v + bias[...], 0.0), row + offset, rows) for v in pair]
        spread_out(target, row, rows, *pair)


def make_merged(state, carried, pieces):
    bias = state.outer1_b[...] + state.out_b[...]
    for (row, rows), pair in zip(pieces, conv(state.x_i, state.outer1_w, pieces), strict=True):
        done = []
        for parity in range(2):
            old = state.kept_r[parity, rows_at(row + 2, rows)].astype(F32)
            value = pair[parity] + bias + old + carried(parity, row, rows)
            state.kept_m[parity, rows_at(row, rows)] = value.astype(BF16)
            done.append(masked(state.mask, jnp.maximum(value, 0.0), row + 3, rows))
        spread_out(state.x_m, row, rows, *done)


def make_united(state, fine, row, outs):
    own, _ = place()
    pair = conv(state.x_n, state.outer2_w, [(row, 4)])[0]
    for parity in range(2):
        old = state.kept_m[parity, rows_at(row + 2, 4)].astype(F32)
        value = pair[parity] + state.outer2_b[...] + old
        for r in range(4):
            cells = value[r * SLOT + HALO : r * SLOT + HALO + SEG]
            for half in range(fine.shape[0]):
                fine[half, pl.ds(r * 2 * SEG + parity, SEG, 2), :] = cells[
                    :, half * 128 : (half + 1) * 128
                ]
    core = lax.rem(own, 2)
    for j in range(2):
        start = pl.multiple_of(lax.bitwise_xor(core, j) * (4 * SEG), 16)
        for half in range(fine.shape[0]):
            value = fine[half, pl.ds(start, 4 * SEG), :].astype(BF16)
            outs[j][:, half * 128 : (half + 1) * 128] = value


class Named:
    def __init__(self, names, refs):
        for name, ref in zip(names, refs, strict=True):
            setattr(self, name, ref)


WEIGHTS = ("lift_w", "merge_w", "inner1_w", "out_w", "outer1_w", "inner2_w", "outer2_w")
BIASES = ("lift_b", "out_b", "inner1_b", "outer1_b", "inner2_b", "outer2_b")
ARRAYS = ("mask", "wide", "x_r", "x_i", "x_m", "kept_r", "kept_m")
LATER = ("x_n", "even_c", "odd_c")


def inner_kernel(blocks, *refs):
    n = len(WEIGHTS)
    block, sources, biases = refs[0], refs[1 : 1 + n], refs[1 + n : 7 + n]
    outs = refs[7 + n : 7 + n + len(ARRAYS) + n]
    window, coarse, thin, sems = refs[-4:]
    state = Named(BIASES + ARRAYS + WEIGHTS, biases + outs)
    own, number = place()
    split = window.shape[1]
    copies = {}
    for i, (name, source) in enumerate(zip(WEIGHTS, sources, strict=True)):
        copies[name] = pltpu.make_async_copy(source, getattr(state, name), sems.at[i])
        copies[name].start()

    slot = lax.broadcasted_iota(jnp.int32, (SLOT, 128), 0)
    token = slot + (own * SEG - HALO)
    inside = (token >= 0) & (token < GW) & (slot < SEG + 2 * HALO)
    inside = jnp.where(inside, 1.0, 0.0)
    for r in range(2 * QUAD + 10):
        at = number * (2 * QUAD) + (r - 5)
        good = jnp.where((at >= 0) & (at < blocks * 2 * QUAD), 1.0, 0.0)
        state.mask[r * SLOT : (r + 1) * SLOT] = inside * good

    for i in range(QUAD):
        there = slice(i * SENT, (i + 1) * SENT)
        for target, cols in ((window, slice(0, split)), (coarse, slice(split, None))):
            target[i * SLOT : i * SLOT + SENT] = block[there, cols]
            blank = jnp.zeros((SLOT - SENT, target.shape[1]), BF16)
            target[i * SLOT + SENT : (i + 1) * SLOT] = blank

    copies["lift_w"].wait()
    tokens = [(0, [5 + 2 * i + a for i in range(QUAD)]) for a in range(2)]
    lift(window, state.lift_w, state.lift_b, state.mask, state.wide, tokens)
    copies["merge_w"].wait()
    make_reassembled(state, [(5, 6)])
    copies["inner1_w"].wait()
    make_inner(state.x_r, state.inner1_w, state.inner1_b, state.mask, state.x_i, 2, [(5, 4)])
    copies["out_w"].wait()
    thin[...] = jnp.dot(coarse[...], state.out_w[...], preferred_element_type=F32)
    copies["outer1_w"].wait()

    def carried(parity, row, rows):
        return jnp.concatenate([enlarged(thin, 0, r - 2)[parity] for r in range(row, row + rows)])

    make_merged(state, carried, [(5, 2)])
    copies["inner2_w"].wait()
    copies["outer2_w"].wait()


def near_kernel(blocks, *refs):
    names = BIASES + WEIGHTS + tuple("old_" + name for name in ARRAYS)
    block, first, second = refs[:3]
    inputs = refs[3 : 3 + len(names)]
    outs = refs[3 + len(names) : -4]
    window, coarse, thin, fine = refs[-4:]
    state = Named(names + ARRAYS + LATER, inputs + outs[: len(ARRAYS) + len(LATER)])
    results = outs[len(ARRAYS) + len(LATER) :]
    own, number = place()
    split, width = window.shape[1], thin.shape[1]

    for target in (window, coarse):
        blank = jnp.zeros((SLOT - SENT, target.shape[1]), BF16)
        for i in range(target.shape[0] // SLOT):
            target[i * SLOT + SENT : (i + 1) * SLOT] = blank
    for i in range(QUAD):
        at = (i + 2) * SLOT
        coarse[at : at + SENT] = block[i * SENT : (i + 1) * SENT, split:]

    def land(payload, row, coarse_row):
        for i in range(HALO):
            at = (row + i) * SLOT
            window[at : at + SENT] = payload[i * SENT : (i + 1) * SENT]
        for half in range(2):
            at = (coarse_row + half) * SLOT
            coarse[at : at + SENT] = payload[HALO * SENT :, half * width : (half + 1) * width]

    even_block = lax.rem(number, 2) == 0

    @pl.when(even_block)
    def _():
        land(second, 0, 0)
        land(first, HALO, QUAD + 2)

    @pl.when(jnp.logical_not(even_block))
    def _():
        land(first, 0, 0)
        land(second, HALO, QUAD + 2)

    @pl.when(number == 0)
    def _():
        coarse[SLOT : SLOT + SENT] = block[:SENT, split:]

    @pl.when(number == blocks - 1)
    def _():
        at = (QUAD + 2) * SLOT
        coarse[at : at + SENT] = block[(QUAD - 1) * SENT :, split:]

    tokens = [(1, [1, 3, 13, 15, 17]), (0, [0, 2, 4, 14, 16])]
    lift(window, state.lift_w, state.lift_b, state.mask, state.wide, tokens)
    thin[...] = jnp.dot(coarse[...], state.out_w[...], preferred_element_type=F32)
    for row in range(2 * QUAD + 4):
        left, right = enlarged(thin, -2, row - 2)
        state.even_c[row * SLOT : (row + 1) * SLOT] = left
        state.odd_c[row * SLOT : (row + 1) * SLOT] = right

    def carried(parity, row, rows):
        return (state.even_c, state.odd_c)[parity][rows_at(row, rows)]

    other = 1 - lax.div(own, 2)
    single, run = 11 - 7 * other, 11 * other
    pieces = [(single, 1), (run, 5)]
    make_reassembled(state, pieces)
    pieces = [(9 - 5 * other, 1), (9 * other, 5)]
    make_inner(state.x_r, state.inner1_w, state.inner1_b, state.mask, state.x_i, 2, pieces)
    pieces = [(7 - 3 * other, 1), (7 * other, 5)]
    make_merged(state, carried, pieces)
    pieces = [(4 * other, 6)]
    make_inner(state.x_m, state.inner2_w, state.inner2_b, state.mask, state.x_n, 4, pieces)
    make_united(state, fine, 4 * other, results)


def own_kernel(*refs):
    arrays = ARRAYS + LATER
    names = BIASES + WEIGHTS + tuple("old_" + name for name in arrays)
    inputs, outs, fine = refs[: len(names)], refs[len(names) : -1], refs[-1]
    state = Named(names + arrays, inputs + outs[: len(arrays)])
    own, _ = place()

    def carried(parity, row, rows):
        return (state.even_c, state.odd_c)[parity][rows_at(row, rows)]

    mine = lax.div(own, 2)
    make_reassembled(state, [(12 * mine, 4)])
    pieces = [(10 * mine, 4)]
    make_inner(state.x_r, state.inner1_w, state.inner1_b, state.mask, state.x_i, 2, pieces)
    make_merged(state, carried, [(8 * mine, 4)])
    pieces = [(6 * mine, 4)]
    make_inner(state.x_m, state.inner2_w, state.inner2_b, state.mask, state.x_n, 4, pieces)
    make_united(state, fine, 4 * mine, outs[len(arrays) :])


def assemble_kernel(*refs):
    pieces, out = refs[:QUAD], refs[QUAD]
    own, _ = place()
    for k in range(QUAD):
        start = pl.multiple_of(lax.bitwise_xor(own, k) * (2 * SEG), 16)
        for r in range(2):
            out[r, pl.ds(start, 2 * SEG), :] = pieces[k][r * 2 * SEG : (r + 1) * 2 * SEG]


def body(
    tap_two,
    coarse_path,
    proj_weight,
    proj_bias,
    lift_weight,
    lift_bias,
    merge_weight,
    out_weight,
    out_bias,
    first_inner_w,
    first_inner_b,
    first_outer_w,
    first_outer_b,
    second_inner_w,
    second_inner_b,
    second_outer_w,
    second_outer_b,
):
    count = lax.axis_size("rows")
    if tap_two.shape[0] != GW or count % QUAD:
        raise ValueError("unsupported split")
    blocks = count // QUAD
    split = proj_weight.shape[1]
    width = out_weight.shape[1]
    shape = jax.ShapeDtypeStruct
    hbm = functools.partial(pltpu.with_memory_space_constraint, memory_space=pltpu.HBM)

    def swap(value, k):
        return lax.ppermute(value, "rows", [(i, i ^ k) for i in range(count)])

    def between(value, parity):
        pairs = []
        for low in range(parity, blocks - 1, 2):
            for q in range(QUAD):
                a, b = low * QUAD + q, (low + 1) * QUAD + q
                pairs += [(a, b), (b, a)]
        return lax.ppermute(value, "rows", pairs)

    segments = pl.pallas_call(
        project_kernel,
        out_shape=[shape((SENT, split + width), BF16)] * QUAD,
        in_specs=[HBM] * 4,
        out_specs=[VMEM] * QUAD,
        scratch_shapes=[
            pltpu.VMEM((GW + 16, split), F32),
            pltpu.VMEM((GW + 16, width), F32),
            pltpu.VMEM(tap_two.shape, BF16),
            pltpu.VMEM(coarse_path.shape, BF16),
            pltpu.VMEM(proj_weight.shape, BF16),
            pltpu.VMEM((1, split), F32),
            pltpu.SemaphoreType.DMA((4,)),
        ],
        compiler_params=pltpu.CompilerParams(vmem_limit_bytes=8 * MIB),
    )(hbm(tap_two), hbm(coarse_path), hbm(proj_weight), hbm(proj_bias[None]))
    segments = [segments[0]] + [swap(segments[k], k) for k in range(1, QUAD)]
    block, first, second = pl.pallas_call(
        functools.partial(pack_kernel, split),
        out_shape=[shape((QUAD * SENT, split + width), BF16)]
        + [shape(((HALO + 1) * SENT, split), BF16)] * 2,
        in_specs=[VMEM] * QUAD,
        out_specs=[VMEM] * 3,
        compiler_params=pltpu.CompilerParams(vmem_limit_bytes=4 * MIB),
    )(*segments)
    first, second = between(first, 0), between(second, 1)

    weights = (
        lift_weight,
        merge_weight,
        first_inner_w,
        out_weight,
        first_outer_w,
        second_inner_w,
        second_outer_w,
    )
    biases = (lift_bias, out_bias, first_inner_b, first_outer_b, second_inner_b, second_outer_b)
    biases = [bias[None] for bias in biases]
    rows_w = 2 * QUAD + 10
    arrays = [
        pltpu.VMEM((rows_w * SLOT, 128), F32),
        pltpu.VMEM((rows_w * SLOT, 4 * split), BF16),
        pltpu.VMEM(((rows_w - 2) * SLOT, 4 * width), BF16),
        pltpu.VMEM(((rows_w - 4) * SLOT, 4 * width), BF16),
        pltpu.VMEM(((rows_w - 6) * SLOT, 4 * width), BF16),
        pltpu.VMEM((2, (rows_w - 2) * SLOT, width), BF16),
        pltpu.VMEM((2, (rows_w - 6) * SLOT, width), BF16),
    ]
    later = [
        pltpu.VMEM(((rows_w - 8) * SLOT, 4 * width), BF16),
        pltpu.VMEM(((rows_w - 6) * SLOT, width), F32),
        pltpu.VMEM(((rows_w - 6) * SLOT, width), F32),
    ]
    results = [shape((4 * SEG, width), BF16)] * 2

    def cost(lift_rows, merge_rows, rest_rows):
        cells = 2 * SLOT * 2 * split * lift_rows * split
        cells += 2 * 2 * SLOT * 9 * width * (split * merge_rows + width * rest_rows)
        return pl.CostEstimate(flops=cells, bytes_accessed=1_000_000, transcendentals=0)

    def limit(mib):
        return pltpu.CompilerParams(vmem_limit_bytes=mib * MIB)

    made = pl.pallas_call(
        functools.partial(inner_kernel, blocks),
        out_shape=arrays + [pltpu.VMEM(w.shape, BF16) for w in weights],
        in_specs=[VMEM] + [HBM] * len(weights) + [VMEM] * len(biases),
        out_specs=[VMEM] * (len(arrays) + len(weights)),
        scratch_shapes=[
            pltpu.VMEM((QUAD * SLOT, split), BF16),
            pltpu.VMEM((QUAD * SLOT, width), BF16),
            pltpu.VMEM((QUAD * SLOT, width), F32),
            pltpu.SemaphoreType.DMA((len(weights),)),
        ],
        compiler_params=limit(16),
        cost_estimate=cost(8, 6, 6),
    )(block, *[hbm(w) for w in weights], *biases)
    made, weights = made[: len(arrays)], made[len(arrays) :]
    before = 3 + len(biases) + len(weights)
    made = pl.pallas_call(
        functools.partial(near_kernel, blocks),
        out_shape=arrays + later + results,
        in_specs=[VMEM] * (before + len(arrays)),
        out_specs=[VMEM] * (len(arrays) + len(later) + 2),
        scratch_shapes=[
            pltpu.VMEM((2 * HALO * SLOT, split), BF16),
            pltpu.VMEM(((QUAD + 4) * SLOT, width), BF16),
            pltpu.VMEM(((QUAD + 4) * SLOT, width), F32),
            pltpu.VMEM((width // 128, 8 * SEG, 128), F32),
        ],
        input_output_aliases={before + i: i for i in range(len(arrays))},
        compiler_params=limit(16),
        cost_estimate=cost(10, 6, 22),
    )(block, first, second, *biases, *weights, *made)
    arrays += later
    made, far = made[:-2], made[-2:]
    far = [swap(far[j], 2 + j) for j in range(2)]
    before = len(biases) + len(weights)
    made = pl.pallas_call(
        own_kernel,
        out_shape=arrays + results,
        in_specs=[VMEM] * (before + len(arrays)),
        out_specs=[VMEM] * (len(arrays) + 2),
        scratch_shapes=[pltpu.VMEM((width // 128, 8 * SEG, 128), F32)],
        input_output_aliases={before + i: i for i in range(len(arrays))},
        compiler_params=limit(16),
        cost_estimate=cost(0, 4, 16),
    )(*biases, *weights, *made)
    pieces = [made[-2], swap(made[-1], 1), *far]
    return pl.pallas_call(
        assemble_kernel,
        out_shape=shape((2, 2 * GW, width), BF16),
        in_specs=[VMEM] * QUAD,
        out_specs=VMEM,
        compiler_params=pltpu.CompilerParams(vmem_limit_bytes=4 * MIB),
    )(*pieces)


def solution(mesh):
    return jax.shard_map(
        body,
        mesh=mesh,
        in_specs=(P(("groups", "rows"), None), P(("groups", "rows"), None)) + (P(),) * 15,
        out_specs=P(("groups", "rows"), None, None),
        check_vma=False,
    )
```
